512 devices in a mesh: seq: 64 (over y, x, core), ch: 8 (over z).
Axes of the slice: x: 4, y: 8, z: 8, core: 2. Of those that a mesh axis runs over, the one named last changes fastest.
Arguments:
- inputs: bfloat16 [256, 32768], P('ch', 'seq'), may hold values from -6 to 6
- proj_weight: bfloat16 [3, 256, 256], P(None, 'ch'), may hold values from -0.5 to 0.5
- short_taps: float32 [256, 3, 3], P('ch'), may hold values from -3 to 3
- skip_gain: float32 [256, 2], P('ch'), may hold values from -1 to 1
- filters: float32 [2, 256, 32768], P(None, 'ch', 'seq'), may hold values from -1 to 1
- out_weight: bfloat16 [256, 256], P('ch'), may hold values from -0.5 to 0.5
Outputs:
- outputs: bfloat16 [256, 32768], P('ch', 'seq')
The draws below stay inside these ranges and needn't reach their ends.
All inputs are finite; a program needn't handle non-finite values.
Results may differ from the reference program's by a relative error of at most 0.007.
Values may be sent and summed in bfloat16 or wider, within the bound.
No kernel may reach another device: no remote copies, remote signals or barrier semaphores. Data moves between devices by JAX's collectives and lax.ppermute only.
A program may use at most 64 MiB of HBM per device.

```python
import math
import jax
import jax.numpy as jnp

D = 256
TOKENS = 32768


def draw_filters(key, part):
    base = jax.random.fold_in(key, 7)
    rate_key, noise_key = jax.random.split(base)
    lowest = math.log(1.0 / TOKENS)
    highest = math.log(1.0 / 32.0)
    noise = jnp.clip(jax.random.normal(noise_key, (2, D, TOKENS), jnp.float32), -4.0, 4.0)
    rates = jnp.exp(jax.random.uniform(rate_key, (2, D, 1), jnp.float32, lowest, highest))
    position = jnp.arange(TOKENS, dtype=jnp.float32)[None, None, :]
    return noise * jnp.exp(-rates * position) * jnp.sqrt(1.0 - jnp.exp(-2.0 * rates))


def with_spikes(values, key, source, target, blocks, factor):
    owner, partner = [(jnp.arange(values.shape[dim]) // (values.shape[dim] // blocks)).reshape([-1 if axis == dim else 1 for axis in range(values.ndim)]) for dim in (source, target)]
    chosen = jax.random.permutation(key, blocks)[partner]
    strong = (owner == chosen) | (owner == (partner + blocks // 2) % blocks)
    return jnp.where(strong, factor * values, values)


def block_levels(key, dims, shards, low, high):
    loudness, own = 1.0, jax.random.fold_in(key, 6)
    for axis_at, blocks in shards:
        steps = jnp.exp(jax.random.uniform(jax.random.fold_in(own, axis_at), (blocks,), jnp.float32, low / len(shards), high / len(shards)))
        loudness = loudness * jnp.repeat(steps, dims[axis_at] // blocks).reshape([-1 if axis == axis_at else 1 for axis in range(len(dims))])
    return loudness


def scatter_about(key, shape, scale, reach, cuts=(), kind=jnp.bfloat16):
    drawn = jax.random.normal(key, shape, jnp.float32) * scale
    if len(cuts) > 0:
        drawn = block_levels(key, shape, cuts, -0.22, 0.18) * drawn
    return jnp.clip(drawn, min=-reach, max=reach).astype(kind)


def noise_with(rng, extent, spread, reach, cuts, heavy, held_as=jnp.bfloat16):
    values = spread * jax.random.normal(rng, extent, jnp.float32)
    if cuts:
        values = values * block_levels(rng, extent, cuts, -0.22, 0.18)
    return jnp.clip(with_spikes(values, jax.random.fold_in(rng, 3), *heavy), -reach, reach).astype(held_as)


def setup_inputs(seed: int = 0) -> dict:
    key_of = jax.random.split(jax.random.key(seed), 7)
    return {
        "inputs": scatter_about(key_of[0], (D, TOKENS), 1.0, 6.0, ((0, 8), (1, 64))),
        "proj_weight": noise_with(key_of[1], (3, D, D), D ** -0.5, 0.5, ((1, 8),), (1, 2, 8, 2.0)),
        "short_taps": scatter_about(key_of[2], (D, 3, 3), 0.6, 3.0, ((0, 8),), jnp.float32),
        "skip_gain": jnp.clip(jax.random.uniform(key_of[3], (D, 2), jnp.float32, -1.0, 1.0) * block_levels(key_of[3], (D, 2), ((0, 8),), -0.4, 0.0), -1.0, 1.0),
        "filters": draw_filters(jax.random.fold_in(key_of[6], 71), 0),
        "out_weight": noise_with(key_of[5], (D, D), D ** -0.5, 0.5, ((0, 8),), (0, 1, 8, 2.0)),
    }


def causal_filter(response, signal):
    width = 2 * signal.shape[-1]
    spectrum = jnp.fft.rfft(response, n=width, axis=-1) * jnp.fft.rfft(signal, n=width, axis=-1)
    return jnp.fft.irfft(spectrum, n=width, axis=-1)[:, :signal.shape[-1]].astype(response.dtype)


def reference(inputs, proj_weight, short_taps, skip_gain, filters, out_weight):
    summed = jnp.einsum('sio,it->ost', proj_weight.astype(jnp.float32), inputs.astype(jnp.float32))
    projected = summed.astype(jnp.bfloat16)
    length = inputs.shape[1]
    zeros_head = jnp.zeros((projected.shape[0], 3, 2), jnp.bfloat16)
    padded = jnp.concatenate([zeros_head, projected], axis=2).astype(jnp.float32)
    conv_in = (short_taps[:, :, 0:1] * padded[:, :, 2:] + short_taps[:, :, 1:2] * padded[:, :, 1:-1]
               + short_taps[:, :, 2:3] * padded[:, :, :-2])
    values = conv_in[:, 0, :]
    first_gate = conv_in[:, 1, :]
    second_gate = conv_in[:, 2, :]
    first = causal_filter(filters[0], values) + skip_gain[:, 0:1] * values
    gated = first_gate * first
    second = causal_filter(filters[1], gated) + skip_gain[:, 1:2] * gated
    mixed = (second_gate * second).astype(jnp.bfloat16)
    result = jnp.dot(out_weight.T, mixed, preferred_element_type=jnp.float32)
    return result.astype(jnp.bfloat16)
```

```python
import functools

import jax
import jax.numpy as jnp
import numpy as np
from jax import lax
from jax.experimental import pallas as pl
from jax.experimental.pallas import tpu as pltpu
from jax.sharding import PartitionSpec as P

bf16 = jnp.bfloat16
f32 = jnp.float32

ROWS = 128
COLS = 256
TOTAL = ROWS * COLS
PLANE = 32
GROUPS = 8
BLOCK = 512


def split(values):
    high = values.astype(bf16)
    return high, (values - high.astype(f32)).astype(bf16)


def halves(table):
    table = np.asarray(table, np.float32)
    high = table.astype(jnp.bfloat16)
    low = (table - high.astype(np.float32)).astype(jnp.bfloat16)
    return high, low


@functools.cache
def tables():
    row = (4 * np.arange(PLANE)[None, :] + np.arange(4)[:, None]).reshape(-1).astype(np.float64)
    freq = 4.0 * np.arange(ROWS) + 1.0
    angle = 2.0 * np.pi * ((freq[:, None] * row[None, :]) % (4 * ROWS)) / (4 * ROWS)
    first = np.concatenate([np.cos(angle), -np.sin(angle)], axis=0)
    column = np.arange(COLS, dtype=np.float64)
    turn = 2.0 * np.pi * ((freq[:, None] * column[None, :]) % (4 * TOTAL)) / (4 * TOTAL)
    twiddle = np.stack([np.cos(turn), -np.sin(turn)]).astype(np.float32)
    inner = 2.0 * np.pi * ((column[:, None] * column[None, :]) % COLS) / COLS
    second = np.concatenate([np.cos(inner), np.sin(inner)], axis=1)
    return {
        "first": np.stack(halves(first)),
        "last": np.stack(halves(first.T / TOTAL)),
        "twiddle": twiddle,
        "second": np.stack(halves(second)),
    }


def interleave(outer, inner):
    table = np.zeros((outer * inner, outer * inner), np.float32)
    for a in range(outer):
        for b in range(inner):
            table[a * inner + b, b * outer + a] = 1.0
    return table.astype(jnp.bfloat16)


def mm(left, right):
    return jnp.dot(left, right, preferred_element_type=f32)


def left_product(table, values):
    high, low = split(values)
    return mm(table[0], high) + mm(table[0], low) + mm(table[1], high)


def right_product(values, table):
    high, low = split(values)
    return mm(high, table[0]) + mm(low, table[0]) + mm(high, table[1])


def pack_kernel(x_ref, proj_ref, out_w_ref, o_ref):
    x = x_ref[...]
    weights = [proj_ref[g].astype(f32) for g in range(3)] + [out_w_ref[...].astype(f32)]
    lane = lax.broadcasted_iota(jnp.int32, (32, 128), 1) // 32
    for z in range(GROUPS):
        tile, offset = z // 4, z % 4
        picked = None
        for g in range(4):
            piece = weights[g][:, 128 * tile : 128 * tile + 128]
            by = (32 * (g - offset)) % 128
            if by:
                piece = pltpu.roll(piece, by, 1)
            picked = piece if picked is None else jnp.where(lane == g, piece, picked)
        o_ref[z, :, 0:BLOCK] = x
        o_ref[z, :, BLOCK : BLOCK + 128] = picked.astype(bf16)


def project_kernel(r_ref, filters_ref, perm_ref, o_ref):
    x = r_ref[:, 0:BLOCK]
    weights = r_ref[:, BLOCK : BLOCK + 128]
    projected = lax.dot_general(
        weights, x, (((0,), (0,)), ((), ())), preferred_element_type=f32
    ).astype(bf16)
    filters = jnp.concatenate([filters_ref[0], filters_ref[1]], axis=0)
    high, low = split(filters)
    stacked = jnp.concatenate([projected, high, low], axis=0)
    o_ref[...] = mm(perm_ref[...], stacked).astype(bf16)


def forward(signals, first, twiddle, second):
    count = len(signals)
    stage = left_product(first, jnp.concatenate(signals, axis=1))
    rows = []
    for s in range(count):
        real = stage[:ROWS, COLS * s : COLS * (s + 1)]
        imag = stage[ROWS:, COLS * s : COLS * (s + 1)]
        rows.append(real * twiddle[0] - imag * twiddle[1])
        rows.append(real * twiddle[1] + imag * twiddle[0])
    product = right_product(jnp.concatenate(rows, axis=0), second)
    spectra = []
    for s in range(count):
        real = product[2 * ROWS * s : 2 * ROWS * s + ROWS]
        imag = product[2 * ROWS * s + ROWS : 2 * ROWS * (s + 1)]
        spectra.append((real[:, :COLS] + imag[:, COLS:], imag[:, :COLS] - real[:, COLS:]))
    return spectra


def inverse(spectrum, last, twiddle, second):
    product = right_product(jnp.concatenate(spectrum, axis=0), second)
    real = product[:ROWS, :COLS] - product[ROWS:, COLS:]
    imag = product[ROWS:, :COLS] + product[:ROWS, COLS:]
    turned_real = real * twiddle[0] + imag * twiddle[1]
    turned_imag = imag * twiddle[0] - real * twiddle[1]
    return left_product(last, jnp.concatenate([turned_real, turned_imag], axis=0))


def times(left, right):
    return (left[0] * right[0] - left[1] * right[1], left[0] * right[1] + left[1] * right[0])


def short_filter(blocks, taps, group):
    lane = lax.broadcasted_iota(jnp.int32, (PLANE, COLS), 1)
    chip = lax.broadcasted_iota(jnp.int32, (PLANE, COLS), 0)
    shifted = []
    for by in (1, 2):
        rolled = [pltpu.roll(block, by, 1) for block in blocks]
        before = jnp.where(chip == 0, 0.0, pltpu.roll(rolled[3], 1, 0))
        edges = [before, rolled[0], rolled[1], rolled[2]]
        shifted.append([jnp.where(lane < by, edges[q], rolled[q]) for q in range(4)])
    tap = [taps[group : group + 1, j : j + 1] for j in range(3)]
    return [
        tap[0] * blocks[q] + tap[1] * shifted[0][q] + tap[2] * shifted[1][q] for q in range(4)
    ]


def convolve(core, mine, other, taps, gains, perm, first, last, own_last, twiddle, second, spread):
    parts = [
        mm(perm, jnp.where(core == 0, mine, other)),
        mm(perm, jnp.where(core == 0, other, mine)),
    ]

    def classes(slot):
        return [
            parts[q // 2][PLANE * slot : PLANE * (slot + 1), COLS * (q % 2) : COLS * (q % 2 + 1)]
            for q in range(4)
        ]

    groups = [jnp.concatenate(short_filter(classes(g), taps, g), axis=0) for g in range(3)]
    responses = [
        jnp.concatenate(classes(4 + f), axis=0) + jnp.concatenate(classes(6 + f), axis=0)
        for f in range(2)
    ]
    values, first_gate, second_gate = groups
    value_spectrum, first_spectrum, second_spectrum = forward(
        [values] + responses, first, twiddle, second
    )
    convolved = inverse(times(value_spectrum, first_spectrum), last, twiddle, second)
    gated = first_gate * (convolved + gains[:, 0:1] * values)
    (gated_spectrum,) = forward([gated], first, twiddle, second)
    own = inverse(times(gated_spectrum, second_spectrum), own_last, twiddle, second)
    half = ROWS // 2
    own_gated = jnp.where(core == 0, gated[:half], gated[half:])
    own_gate = jnp.where(core == 0, second_gate[:half], second_gate[half:])
    mixed = (own_gate * (own + gains[:, 1:2] * own_gated)).astype(bf16)
    lanes = jnp.concatenate(
        [
            mixed[PLANE * (j // 2) : PLANE * (j // 2 + 1), 128 * (j % 2) : 128 * (j % 2 + 1)]
            for j in range(4)
        ],
        axis=0,
    )
    return mm(spread, lanes).astype(bf16)


def convolve_kernel(
    mine_ref, other_ref, taps_ref, gains_ref, perm_ref, first_ref, last_ref, twiddle_ref,
    second_ref, spread_ref, o_ref,
):
    device = lax.axis_index("seq")
    core = device % 2
    channel = device // 2
    half = ROWS // 2
    out = convolve(
        core,
        mine_ref[...],
        other_ref[...],
        taps_ref[channel],
        gains_ref[pl.ds(channel, 1), :],
        perm_ref[...],
        first_ref,
        last_ref,
        [last_ref[i, pl.ds(pl.multiple_of(half * core, half), half), :] for i in range(2)],
        twiddle_ref,
        second_ref,
        spread_ref[...],
    )
    for z in range(GROUPS):
        o_ref[z] = out


def output_kernel(r_ref, weights_ref, o_ref, scratch):
    scratch[...] = r_ref[...].astype(f32)
    mixed = jnp.concatenate(
        [scratch[pl.ds(j, 256, stride=4), :].astype(bf16) for j in range(4)], axis=1
    )
    weights = weights_ref[:, 96:128]
    o_ref[...] = lax.dot_general(
        weights, mixed, (((0,), (0,)), ((), ())), preferred_element_type=f32
    ).astype(bf16)


def local(inputs, proj_weight, short_taps, skip_gain, filters, out_weight):
    table = tables()
    packed = pl.pallas_call(
        pack_kernel,
        out_shape=jax.ShapeDtypeStruct((GROUPS, 32, BLOCK + 128), bf16),
        name="pack",
    )(inputs, proj_weight, out_weight)
    gathered = lax.all_to_all(packed, "ch", 0, 0, tiled=True).reshape(256, BLOCK + 128)

    perm = interleave(PLANE, 8)
    sent = pl.pallas_call(
        project_kernel,
        out_shape=jax.ShapeDtypeStruct((256, BLOCK), bf16),
        name="project",
    )(gathered, filters, perm)
    same_core = [[2 * c + k for c in range(PLANE)] for k in range(2)]
    mine = lax.all_to_all(
        sent.reshape(PLANE, 8, BLOCK), "seq", 0, 0, tiled=True, axis_index_groups=same_core
    ).reshape(256, BLOCK)
    other = lax.ppermute(mine, "seq", [(i, i ^ 1) for i in range(2 * PLANE)])

    mixed = pl.pallas_call(
        convolve_kernel,
        out_shape=jax.ShapeDtypeStruct((GROUPS, 128, 128), bf16),
        name="convolve",
    )(
        mine,
        other,
        short_taps,
        skip_gain,
        np.ascontiguousarray(perm.T),
        table["first"],
        table["last"],
        table["twiddle"],
        table["second"],
        interleave(PLANE, 4),
    )
    everyone = [
        [(2 * c + k) * GROUPS + z for z in range(GROUPS) for c in range(PLANE)] for k in range(2)
    ]
    arrived = lax.all_to_all(
        mixed.reshape(256, 4, 128),
        ("seq", "ch"),
        0,
        0,
        tiled=True,
        axis_index_groups=everyone,
    ).reshape(1024, 128)
    return pl.pallas_call(
        output_kernel,
        out_shape=jax.ShapeDtypeStruct((32, BLOCK), bf16),
        in_specs=[
            pl.BlockSpec((1024, 128), lambda i: (0, 0)),
            pl.BlockSpec((256, 128), lambda i: (0, 4)),
        ],
        out_specs=pl.BlockSpec((32, BLOCK), lambda i: (0, 0)),
        grid=(1,),
        scratch_shapes=[pltpu.VMEM((1024, 128), f32)],
        name="output",
    )(arrived, gathered)


def solution(mesh):
    in_specs = (
        P("ch", "seq"),
        P(None, "ch", None),
        P("ch", None, None),
        P("ch", None),
        P(None, "ch", "seq"),
        P("ch", None),
    )
    return jax.shard_map(
        local, mesh=mesh, in_specs=in_specs, out_specs=P("ch", "seq"), check_vma=False
    )
```

```python
import functools

import jax
import jax.numpy as jnp
import numpy as np
from jax import lax
from jax.experimental import pallas as pl
from jax.experimental.pallas import tpu as pltpu
from jax.sharding import PartitionSpec as P

bf16 = jnp.bfloat16
f32 = jnp.float32

ROWS = 128
COLS = 256
TOTAL = ROWS * COLS
PLANE = 32
GROUPS = 8
BLOCK = 512
CHUNK = 20


def split(values):
    high = values.astype(bf16)
    return high, (values - high.astype(f32)).astype(bf16)


def halves(table):
    table = np.asarray(table, np.float32)
    high = table.astype(jnp.bfloat16)
    low = (table - high.astype(np.float32)).astype(jnp.bfloat16)
    return high, low


@functools.cache
def tables():
    row = (4 * np.arange(PLANE)[None, :] + np.arange(4)[:, None]).reshape(-1).astype(np.float64)
    freq = 4.0 * np.arange(ROWS) + 1.0
    angle = 2.0 * np.pi * ((freq[:, None] * row[None, :]) % (4 * ROWS)) / (4 * ROWS)
    first = np.concatenate([np.cos(angle), -np.sin(angle)], axis=0)
    column = np.arange(COLS, dtype=np.float64)
    turn = 2.0 * np.pi * ((freq[:, None] * column[None, :]) % (4 * TOTAL)) / (4 * TOTAL)
    inner = 2.0 * np.pi * ((column[:, None] * column[None, :]) % COLS) / COLS
    cosine, sine = np.cos(inner), np.sin(inner)
    high, low = halves(first)
    return {
        "first": np.stack(
            [np.concatenate([high, high], axis=1), np.concatenate([high, low], axis=1)]
        ),
        "last": np.stack(halves(first.T / TOTAL)),
        "twiddle": np.stack([np.cos(turn), -np.sin(turn)]).astype(np.float32),
        "second": np.stack([np.stack(halves(t)) for t in (cosine, cosine + sine, cosine - sine)]),
    }


def mm(left, right):
    return jnp.dot(left, right, preferred_element_type=f32)


def left_product(table, values):
    high, low = split(values)
    return mm(table[0], high) + mm(table[0], low) + mm(table[1], high)


def right_product(values, table):
    high, low = split(values)
    return mm(high, table[0]) + mm(low, table[0]) + mm(high, table[1])


def pack_kernel(x_hbm, proj_hbm, out_w_hbm, o_ref, x_ref, proj_ref, out_w_ref, sems):
    copies = [
        pltpu.make_async_copy(proj_hbm, proj_ref, sems.at[0]),
        pltpu.make_async_copy(out_w_hbm, out_w_ref, sems.at[1]),
        pltpu.make_async_copy(x_hbm, x_ref, sems.at[2]),
    ]
    for copy in copies:
        copy.start()
    copies[0].wait()
    copies[1].wait()
    weights = [proj_ref[g].astype(f32) for g in range(3)] + [out_w_ref[...].astype(f32)]
    lane = lax.broadcasted_iota(jnp.int32, (32, 128), 1) // 32
    for z in range(GROUPS):
        tile, offset = z // 4, z % 4
        picked = None
        for g in range(4):
            piece = weights[g][:, 128 * tile : 128 * tile + 128]
            by = (32 * (g - offset)) % 128
            if by:
                piece = pltpu.roll(piece, by, 1)
            picked = piece if picked is None else jnp.where(lane == g, piece, picked)
        o_ref[z, :, BLOCK : BLOCK + 128] = picked.astype(bf16)
    copies[2].wait()
    x = x_ref[...]
    for z in range(GROUPS):
        o_ref[z, :, 0:BLOCK] = x


def project_kernel(r_ref, filters_ref, o_ref, scratch):
    x = r_ref[:, 0:BLOCK]
    weights = r_ref[:, BLOCK : BLOCK + 128]
    projected = lax.dot_general(
        weights, x, (((0,), (0,)), ((), ())), preferred_element_type=f32
    )
    for j in range(4):
        lanes = slice(128 * j, 128 * (j + 1))
        for g in range(3):
            scratch[pl.ds(4 * g + j, PLANE, stride=CHUNK), :] = projected[
                PLANE * g : PLANE * (g + 1), lanes
            ]
        for f in range(2):
            scratch[pl.ds(12 + 4 * f + j, PLANE, stride=CHUNK), :] = filters_ref[f, :, lanes]
    o_ref[...] = scratch[...].astype(bf16)


def outer_forward(signal, first):
    high, low = split(signal)
    return mm(first[0], jnp.concatenate([high, low], axis=0)) + mm(first[1][:, ROWS:], high)


def inner_forward(stages, twiddle, second):
    reals, imags = [], []
    for stage in stages:
        real, imag = stage[:ROWS], stage[ROWS:]
        reals.append(real * twiddle[0] - imag * twiddle[1])
        imags.append(real * twiddle[1] + imag * twiddle[0])
    real = jnp.concatenate(reals, axis=0)
    imag = jnp.concatenate(imags, axis=0)
    both = right_product(real + imag, second[0])
    out_real = both - right_product(imag, second[2])
    out_imag = both - right_product(real, second[1])
    return [
        (out_real[ROWS * s : ROWS * (s + 1)], out_imag[ROWS * s : ROWS * (s + 1)])
        for s in range(len(stages))
    ]


def inverse(spectrum, last, twiddle, second):
    both = right_product(spectrum[0] + spectrum[1], second[0])
    real = both - right_product(spectrum[1], second[1])
    imag = both - right_product(spectrum[0], second[2])
    turned_real = real * twiddle[0] + imag * twiddle[1]
    turned_imag = imag * twiddle[0] - real * twiddle[1]
    return left_product(last, jnp.concatenate([turned_real, turned_imag], axis=0))


def times(left, right):
    return (left[0] * right[0] - left[1] * right[1], left[0] * right[1] + left[1] * right[0])


def short_filter(blocks, taps, group):
    lane = lax.broadcasted_iota(jnp.int32, (PLANE, COLS), 1)
    chip = lax.broadcasted_iota(jnp.int32, (PLANE, COLS), 0)
    shifted = []
    for by in (1, 2):
        rolled = [pltpu.roll(block, by, 1) for block in blocks]
        before = jnp.where(chip == 0, 0.0, pltpu.roll(rolled[3], 1, 0))
        edges = [before, rolled[0], rolled[1], rolled[2]]
        shifted.append([jnp.where(lane < by, edges[q], rolled[q]) for q in range(4)])
    tap = [taps[group : group + 1, j : j + 1] for j in range(3)]
    return [
        tap[0] * blocks[q] + tap[1] * shifted[0][q] + tap[2] * shifted[1][q] for q in range(4)
    ]


def convolve(core, loaded, taps, gains, first, last, own_last, twiddle, second):
    def classes(array):
        return [
            jnp.concatenate([loaded(q // 2, array, 2 * (q % 2) + h) for h in range(2)], axis=1)
            for q in range(4)
        ]

    groups = [jnp.concatenate(short_filter(classes(g), taps, g), axis=0) for g in range(3)]
    responses = jnp.concatenate(
        [jnp.concatenate(classes(3 + f), axis=0).astype(bf16) for f in range(2)], axis=1
    )
    values, first_gate, second_gate = groups
    pair = mm(first[1], jnp.concatenate([responses, responses], axis=0))
    value_spectrum, first_spectrum, second_spectrum = inner_forward(
        [outer_forward(values, first), pair[:, :COLS], pair[:, COLS:]], twiddle, second
    )
    convolved = inverse(times(value_spectrum, first_spectrum), last, twiddle, second)
    gated = first_gate * (convolved + gains[:, 0:1] * values)
    (gated_spectrum,) = inner_forward([outer_forward(gated, first)], twiddle, second)
    own = inverse(times(gated_spectrum, second_spectrum), own_last, twiddle, second)
    half = ROWS // 2
    own_gated = jnp.where(core == 0, gated[:half], gated[half:])
    own_gate = jnp.where(core == 0, second_gate[:half], second_gate[half:])
    return own_gate * (own + gains[:, 1:2] * own_gated)


def convolve_kernel(
    mine_ref, other_ref, taps_ref, gains_ref, first_ref, last_ref, twiddle_ref, second_ref,
    o_ref, wide, result,
):
    device = lax.axis_index("seq")
    core = device % 2
    channel = device // 2
    half = ROWS // 2
    wide[core] = mine_ref[...].astype(f32)
    wide[1 - core] = other_ref[...].astype(f32)
    mixed = convolve(
        core,
        lambda k, array, j: wide[k, pl.ds(4 * array + j, PLANE, stride=CHUNK), :],
        taps_ref[channel],
        gains_ref[pl.ds(channel, 1), :],
        first_ref,
        last_ref,
        [last_ref[i, pl.ds(pl.multiple_of(half * core, half), half), :] for i in range(2)],
        twiddle_ref,
        second_ref,
    )
    for j in range(4):
        result[pl.ds(j, PLANE, stride=4), :] = mixed[
            PLANE * (j // 2) : PLANE * (j // 2 + 1), 128 * (j % 2) : 128 * (j % 2 + 1)
        ]
    out = result[...].astype(bf16)
    for z in range(GROUPS):
        o_ref[z] = out


def output_kernel(r_ref, weights_ref, o_ref, scratch):
    scratch[...] = r_ref[...].astype(f32)
    mixed = jnp.concatenate(
        [scratch[pl.ds(j, 256, stride=4), :].astype(bf16) for j in range(4)], axis=1
    )
    weights = weights_ref[:, 96:128]
    o_ref[...] = lax.dot_general(
        weights, mixed, (((0,), (0,)), ((), ())), preferred_element_type=f32
    ).astype(bf16)


def grant(mebibytes):
    return pltpu.CompilerParams(vmem_limit_bytes=mebibytes * 1024 * 1024)


def local(inputs, proj_weight, short_taps, skip_gain, filters, out_weight):
    table = tables()
    hbm = pl.BlockSpec(memory_space=pltpu.HBM)
    packed = pl.pallas_call(
        pack_kernel,
        out_shape=jax.ShapeDtypeStruct((GROUPS, 32, BLOCK + 128), bf16),
        in_specs=[hbm] * 3,
        scratch_shapes=[
            pltpu.VMEM((32, BLOCK), bf16),
            pltpu.VMEM((3, 32, 256), bf16),
            pltpu.VMEM((32, 256), bf16),
            pltpu.SemaphoreType.DMA((3,)),
        ],
        compiler_params=grant(4),
        name="pack",
    )(inputs, proj_weight, out_weight)
    gathered = lax.all_to_all(packed, "ch", 0, 0, tiled=True).reshape(256, BLOCK + 128)

    sent = pl.pallas_call(
        project_kernel,
        out_shape=jax.ShapeDtypeStruct((PLANE * CHUNK, 128), bf16),
        scratch_shapes=[pltpu.VMEM((PLANE * CHUNK, 128), f32)],
        compiler_params=grant(8),
        name="project",
    )(gathered, filters)
    same_core = [[2 * c + k for c in range(PLANE)] for k in range(2)]
    mine = lax.all_to_all(
        sent.reshape(PLANE, CHUNK // 4, 4, 128),
        "seq",
        0,
        0,
        tiled=True,
        axis_index_groups=same_core,
    ).reshape(PLANE * CHUNK, 128)
    other = lax.ppermute(mine, "seq", [(i, i ^ 1) for i in range(2 * PLANE)])

    mixed = pl.pallas_call(
        convolve_kernel,
        out_shape=jax.ShapeDtypeStruct((GROUPS, 128, 128), bf16),
        scratch_shapes=[
            pltpu.VMEM((2, PLANE * CHUNK, 128), f32),
            pltpu.VMEM((128, 128), f32),
        ],
        compiler_params=grant(24),
        name="convolve",
    )(
        mine,
        other,
        short_taps,
        skip_gain,
        table["first"],
        table["last"],
        table["twiddle"],
        table["second"],
    )
    everyone = [
        [(2 * c + k) * GROUPS + z for z in range(GROUPS) for c in range(PLANE)] for k in range(2)
    ]
    arrived = lax.all_to_all(
        mixed.reshape(256, 4, 128),
        ("seq", "ch"),
        0,
        0,
        tiled=True,
        axis_index_groups=everyone,
    ).reshape(1024, 128)
    return pl.pallas_call(
        output_kernel,
        out_shape=jax.ShapeDtypeStruct((32, BLOCK), bf16),
        in_specs=[
            pl.BlockSpec((1024, 128), lambda i: (0, 0)),
            pl.BlockSpec((256, 128), lambda i: (0, 4)),
        ],
        out_specs=pl.BlockSpec((32, BLOCK), lambda i: (0, 0)),
        grid=(1,),
        scratch_shapes=[pltpu.VMEM((1024, 128), f32)],
        compiler_params=grant(8),
        name="output",
    )(arrived, gathered)


def solution(mesh):
    in_specs = (
        P("ch", "seq"),
        P(None, "ch", None),
        P("ch", None, None),
        P("ch", None),
        P(None, "ch", "seq"),
        P("ch", None),
    )
    return jax.shard_map(
        local, mesh=mesh, in_specs=in_specs, out_specs=P("ch", "seq"), check_vma=False
    )
```

```python
import functools

import jax
import jax.numpy as jnp
import numpy as np
from jax import lax
from jax.experimental import pallas as pl
from jax.experimental.pallas import tpu as pltpu
from jax.sharding import PartitionSpec as P

bf16 = jnp.bfloat16
f32 = jnp.float32

ROWS = 128
COLS = 256
TOTAL = ROWS * COLS
PLANE = 32
GROUPS = 8
BLOCK = 512
CHUNK = 20


def split(values):
    high = values.astype(bf16)
    return high, (values - high.astype(f32)).astype(bf16)


def halves(table):
    table = np.asarray(table, np.float32)
    high = table.astype(jnp.bfloat16)
    low = (table - high.astype(np.float32)).astype(jnp.bfloat16)
    return high, low


@functools.cache
def tables():
    row = (4 * np.arange(PLANE)[None, :] + np.arange(4)[:, None]).reshape(-1).astype(np.float64)
    freq = 4.0 * np.arange(ROWS) + 1.0
    angle = 2.0 * np.pi * ((freq[:, None] * row[None, :]) % (4 * ROWS)) / (4 * ROWS)
    first = np.concatenate([np.cos(angle), -np.sin(angle)], axis=0)
    column = np.arange(COLS, dtype=np.float64)
    turn = 2.0 * np.pi * ((freq[:, None] * column[None, :]) % (4 * TOTAL)) / (4 * TOTAL)
    inner = 2.0 * np.pi * ((column[:, None] * column[None, :]) % COLS) / COLS
    cosine, sine = np.cos(inner), np.sin(inner)
    high, low = halves(first)
    return {
        "first": np.stack(
            [np.concatenate([high, high], axis=1), np.concatenate([high, low], axis=1)]
        ),
        "last": np.stack(halves(first.T / TOTAL)),
        "twiddle": np.stack([np.cos(turn), -np.sin(turn)]).astype(np.float32),
        "second": np.stack([np.stack(halves(t)) for t in (cosine, cosine + sine, cosine - sine)]),
    }


def mm(left, right):
    return jnp.dot(left, right, preferred_element_type=f32)


def left_product(table, values):
    high, low = split(values)
    return mm(table[0], high) + mm(table[0], low) + mm(table[1], high)


def right_product(values, table):
    high, low = split(values)
    return mm(high, table[0]) + mm(low, table[0]) + mm(high, table[1])


def pack_kernel(x_hbm, proj_hbm, out_w_hbm, o_ref, proj_ref, out_w_ref, sems):
    loads = [
        pltpu.make_async_copy(proj_hbm, proj_ref, sems.at[GROUPS]),
        pltpu.make_async_copy(out_w_hbm, out_w_ref, sems.at[GROUPS + 1]),
    ]
    spread = [
        pltpu.make_async_copy(x_hbm, o_ref.at[z, :, pl.ds(0, BLOCK)], sems.at[z])
        for z in range(GROUPS)
    ]
    for copy in loads + spread:
        copy.start()
    for copy in loads:
        copy.wait()
    weights = [proj_ref[g].astype(f32) for g in range(3)] + [out_w_ref[...].astype(f32)]
    lane = lax.broadcasted_iota(jnp.int32, (32, 128), 1) // 32
    for z in range(GROUPS):
        tile, offset = z // 4, z % 4
        picked = None
        for g in range(4):
            piece = weights[g][:, 128 * tile : 128 * tile + 128]
            by = (32 * (g - offset)) % 128
            if by:
                piece = pltpu.roll(piece, by, 1)
            picked = piece if picked is None else jnp.where(lane == g, piece, picked)
        o_ref[z, :, BLOCK : BLOCK + 128] = picked.astype(bf16)
    for copy in spread:
        copy.wait()


def project_kernel(r_ref, filters_ref, o_ref, scratch):
    x = r_ref[:, 0:BLOCK]
    weights = r_ref[:, BLOCK : BLOCK + 128]
    projected = lax.dot_general(
        weights, x, (((0,), (0,)), ((), ())), preferred_element_type=f32
    )
    for j in range(4):
        lanes = slice(128 * j, 128 * (j + 1))
        for g in range(3):
            scratch[pl.ds(4 * g + j, PLANE, stride=CHUNK), :] = projected[
                PLANE * g : PLANE * (g + 1), lanes
            ]
        for f in range(2):
            scratch[pl.ds(12 + 4 * f + j, PLANE, stride=CHUNK), :] = filters_ref[f, :, lanes]
    o_ref[...] = scratch[...].astype(bf16)


def outer_forward(signal, first):
    high, low = split(signal)
    return mm(first[0], jnp.concatenate([high, low], axis=0)) + mm(first[1][:, ROWS:], high)


def inner_forward(stages, twiddle, second):
    reals, imags = [], []
    for stage in stages:
        real, imag = stage[:ROWS], stage[ROWS:]
        reals.append(real * twiddle[0] - imag * twiddle[1])
        imags.append(real * twiddle[1] + imag * twiddle[0])
    real = jnp.concatenate(reals, axis=0)
    imag = jnp.concatenate(imags, axis=0)
    both = right_product(real + imag, second[0])
    out_real = both - right_product(imag, second[2])
    out_imag = both - right_product(real, second[1])
    return [
        (out_real[ROWS * s : ROWS * (s + 1)], out_imag[ROWS * s : ROWS * (s + 1)])
        for s in range(len(stages))
    ]


def inverse(spectrum, last, twiddle, second):
    both = right_product(spectrum[0] + spectrum[1], second[0])
    real = both - right_product(spectrum[1], second[1])
    imag = both - right_product(spectrum[0], second[2])
    turned_real = real * twiddle[0] + imag * twiddle[1]
    turned_imag = imag * twiddle[0] - real * twiddle[1]
    return left_product(last, jnp.concatenate([turned_real, turned_imag], axis=0))


def times(left, right):
    return (left[0] * right[0] - left[1] * right[1], left[0] * right[1] + left[1] * right[0])


def short_filter(blocks, taps, group):
    lane = lax.broadcasted_iota(jnp.int32, (PLANE, COLS), 1)
    chip = lax.broadcasted_iota(jnp.int32, (PLANE, COLS), 0)
    shifted = []
    for by in (1, 2):
        rolled = [pltpu.roll(block, by, 1) for block in blocks]
        before = jnp.where(chip == 0, 0.0, pltpu.roll(rolled[3], 1, 0))
        edges = [before, rolled[0], rolled[1], rolled[2]]
        shifted.append([jnp.where(lane < by, edges[q], rolled[q]) for q in range(4)])
    tap = [taps[group : group + 1, j : j + 1] for j in range(3)]
    return [
        tap[0] * blocks[q] + tap[1] * shifted[0][q] + tap[2] * shifted[1][q] for q in range(4)
    ]


def convolve(core, loaded, taps, gains, first, last, own_last, twiddle, second):
    def classes(array):
        return [
            jnp.concatenate([loaded(q // 2, array, 2 * (q % 2) + h) for h in range(2)], axis=1)
            for q in range(4)
        ]

    groups = [jnp.concatenate(short_filter(classes(g), taps, g), axis=0) for g in range(3)]
    responses = jnp.concatenate(
        [jnp.concatenate(classes(3 + f), axis=0).astype(bf16) for f in range(2)], axis=1
    )
    values, first_gate, second_gate = groups
    pair = mm(first[1], jnp.concatenate([responses, responses], axis=0))
    value_spectrum, first_spectrum, second_spectrum = inner_forward(
        [outer_forward(values, first), pair[:, :COLS], pair[:, COLS:]], twiddle, second
    )
    convolved = inverse(times(value_spectrum, first_spectrum), last, twiddle, second)
    gated = first_gate * (convolved + gains[:, 0:1] * values)
    (gated_spectrum,) = inner_forward([outer_forward(gated, first)], twiddle, second)
    own = inverse(times(gated_spectrum, second_spectrum), own_last, twiddle, second)
    half = ROWS // 2
    own_gated = jnp.where(core == 0, gated[:half], gated[half:])
    own_gate = jnp.where(core == 0, second_gate[:half], second_gate[half:])
    return own_gate * (own + gains[:, 1:2] * own_gated)


def convolve_kernel(
    mine_ref, other_ref, taps_ref, gains_ref, first_ref, last_ref, twiddle_ref, second_ref,
    o_ref, wide, result,
):
    device = lax.axis_index("seq")
    core = device % 2
    channel = device // 2
    half = ROWS // 2
    wide[core] = mine_ref[...].astype(f32)
    wide[1 - core] = other_ref[...].astype(f32)
    mixed = convolve(
        core,
        lambda k, array, j: wide[k, pl.ds(4 * array + j, PLANE, stride=CHUNK), :],
        taps_ref[channel],
        gains_ref[pl.ds(channel, 1), :],
        first_ref,
        last_ref,
        [last_ref[i, pl.ds(pl.multiple_of(half * core, half), half), :] for i in range(2)],
        twiddle_ref,
        second_ref,
    )
    for j in range(4):
        result[pl.ds(j, PLANE, stride=4), :] = mixed[
            PLANE * (j // 2) : PLANE * (j // 2 + 1), 128 * (j % 2) : 128 * (j % 2 + 1)
        ]
    out = result[...].astype(bf16)
    for z in range(GROUPS):
        o_ref[z] = out


def output_kernel(r_ref, weights_ref, o_ref, scratch):
    scratch[...] = r_ref[...].astype(f32)
    mixed = jnp.concatenate(
        [scratch[pl.ds(j, 256, stride=4), :].astype(bf16) for j in range(4)], axis=1
    )
    weights = weights_ref[:, BLOCK + 96 : BLOCK + 128]
    o_ref[...] = lax.dot_general(
        weights, mixed, (((0,), (0,)), ((), ())), preferred_element_type=f32
    ).astype(bf16)


def grant(mebibytes):
    return pltpu.CompilerParams(vmem_limit_bytes=mebibytes * 1024 * 1024)


def local(inputs, proj_weight, short_taps, skip_gain, filters, out_weight):
    table = tables()
    hbm = pl.BlockSpec(memory_space=pltpu.HBM)
    packed = pl.pallas_call(
        pack_kernel,
        out_shape=jax.ShapeDtypeStruct((GROUPS, 32, BLOCK + 128), bf16),
        in_specs=[hbm] * 3,
        scratch_shapes=[
            pltpu.VMEM((3, 32, 256), bf16),
            pltpu.VMEM((32, 256), bf16),
            pltpu.SemaphoreType.DMA((GROUPS + 2,)),
        ],
        compiler_params=grant(4),
        name="pack",
    )(*(pltpu.with_memory_space_constraint(a, pltpu.HBM) for a in (inputs, proj_weight, out_weight)))
    gathered = lax.all_to_all(packed, "ch", 0, 0, tiled=True).reshape(256, BLOCK + 128)

    sent = pl.pallas_call(
        project_kernel,
        out_shape=jax.ShapeDtypeStruct((PLANE * CHUNK, 128), bf16),
        scratch_shapes=[pltpu.VMEM((PLANE * CHUNK, 128), f32)],
        compiler_params=grant(8),
        name="project",
    )(gathered, filters)
    same_core = [[2 * c + k for c in range(PLANE)] for k in range(2)]
    mine = lax.all_to_all(
        sent.reshape(PLANE, CHUNK // 4, 4, 128),
        "seq",
        0,
        0,
        tiled=True,
        axis_index_groups=same_core,
    ).reshape(PLANE * CHUNK, 128)
    other = lax.ppermute(mine, "seq", [(i, i ^ 1) for i in range(2 * PLANE)])

    mixed = pl.pallas_call(
        convolve_kernel,
        out_shape=jax.ShapeDtypeStruct((GROUPS, 128, 128), bf16),
        scratch_shapes=[
            pltpu.VMEM((2, PLANE * CHUNK, 128), f32),
            pltpu.VMEM((128, 128), f32),
        ],
        compiler_params=grant(24),
        name="convolve",
    )(
        mine,
        other,
        short_taps,
        skip_gain,
        table["first"],
        table["last"],
        table["twiddle"],
        table["second"],
    )
    everyone = [
        [(2 * c + k) * GROUPS + z for z in range(GROUPS) for c in range(PLANE)] for k in range(2)
    ]
    arrived = lax.all_to_all(
        mixed.reshape(256, 4, 128),
        ("seq", "ch"),
        0,
        0,
        tiled=True,
        axis_index_groups=everyone,
    ).reshape(1024, 128)
    return pl.pallas_call(
        output_kernel,
        out_shape=jax.ShapeDtypeStruct((32, BLOCK), bf16),
        scratch_shapes=[pltpu.VMEM((1024, 128), f32)],
        compiler_params=grant(8),
        name="output",
    )(arrived, gathered)


def solution(mesh):
    in_specs = (
        P("ch", "seq"),
        P(None, "ch", None),
        P("ch", None, None),
        P("ch", None),
        P(None, "ch", "seq"),
        P("ch", None),
    )
    return jax.shard_map(
        local, mesh=mesh, in_specs=in_specs, out_specs=P("ch", "seq"), check_vma=False
    )
```

```python
import functools

import jax
import jax.numpy as jnp
import numpy as np
from jax import lax
from jax.experimental import pallas as pl
from jax.experimental.pallas import tpu as pltpu
from jax.sharding import PartitionSpec as P

bf16 = jnp.bfloat16
f32 = jnp.float32

ROWS = 128
COLS = 256
TOTAL = ROWS * COLS
HALF = COLS // 2
PLANE = 32
GROUPS = 8
BLOCK = 512
CHUNK = 20


def split(values):
    high = values.astype(bf16)
    return high, (values - high.astype(f32)).astype(bf16)


def halves(table):
    table = np.asarray(table, np.float32)
    high = table.astype(jnp.bfloat16)
    low = (table - high.astype(np.float32)).astype(jnp.bfloat16)
    return high, low


@functools.cache
def tables():
    row = (4 * np.arange(PLANE)[None, :] + np.arange(4)[:, None]).reshape(-1).astype(np.float64)
    freq = 4.0 * np.arange(ROWS) + 1.0
    angle = 2.0 * np.pi * ((freq[:, None] * row[None, :]) % (4 * ROWS)) / (4 * ROWS)
    first = np.concatenate([np.cos(angle), -np.sin(angle)], axis=0)
    column = np.arange(COLS, dtype=np.float64)
    turn = 2.0 * np.pi * ((freq[:, None] * column[None, :]) % (4 * TOTAL)) / (4 * TOTAL)
    part = column[:HALF]
    inner = 2.0 * np.pi * ((part[:, None] * part[None, :]) % HALF) / HALF
    cosine, sine = np.cos(inner), np.sin(inner)
    spin = 2.0 * np.pi * part[None, :] / COLS
    high, low = halves(first)
    return {
        "first": np.stack(
            [np.concatenate([high, high], axis=1), np.concatenate([high, low], axis=1)]
        ),
        "last": np.stack(halves(first.T / TOTAL)),
        "twiddle": np.stack([np.cos(turn), -np.sin(turn)]).astype(np.float32),
        "spin": np.stack([np.cos(spin), -np.sin(spin)]).astype(np.float32),
        "second": np.stack(halves(np.block([[cosine, -sine], [sine, cosine]]))),
    }


def mm(left, right):
    return jnp.dot(left, right, preferred_element_type=f32)


def left_product(table, values):
    high, low = split(values)
    return mm(table[0], high) + mm(table[0], low) + mm(table[1], high)


def right_product(values, table):
    high, low = split(values)
    return mm(high, table[0]) + mm(low, table[0]) + mm(high, table[1])


def pack_kernel(x_hbm, proj_hbm, out_w_hbm, o_ref, proj_ref, out_w_ref, sems):
    loads = [
        pltpu.make_async_copy(proj_hbm, proj_ref, sems.at[GROUPS]),
        pltpu.make_async_copy(out_w_hbm, out_w_ref, sems.at[GROUPS + 1]),
    ]
    spread = [
        pltpu.make_async_copy(x_hbm, o_ref.at[z, :, pl.ds(0, BLOCK)], sems.at[z])
        for z in range(GROUPS)
    ]
    for copy in loads + spread:
        copy.start()
    for copy in loads:
        copy.wait()
    weights = [proj_ref[g].astype(f32) for g in range(3)] + [out_w_ref[...].astype(f32)]
    lane = lax.broadcasted_iota(jnp.int32, (32, 128), 1) // 32
    for z in range(GROUPS):
        tile, offset = z // 4, z % 4
        picked = None
        for g in range(4):
            piece = weights[g][:, 128 * tile : 128 * tile + 128]
            by = (32 * (g - offset)) % 128
            if by:
                piece = pltpu.roll(piece, by, 1)
            picked = piece if picked is None else jnp.where(lane == g, piece, picked)
        o_ref[z, :, BLOCK : BLOCK + 128] = picked.astype(bf16)
    for copy in spread:
        copy.wait()


def project_kernel(r_ref, filters_ref, o_ref, scratch):
    x = r_ref[:, 0:BLOCK]
    weights = r_ref[:, BLOCK : BLOCK + 128]
    projected = lax.dot_general(
        weights, x, (((0,), (0,)), ((), ())), preferred_element_type=f32
    )
    for j in range(4):
        lanes = slice(128 * j, 128 * (j + 1))
        for g in range(3):
            scratch[pl.ds(4 * g + j, PLANE, stride=CHUNK), :] = projected[
                PLANE * g : PLANE * (g + 1), lanes
            ]
        for f in range(2):
            scratch[pl.ds(12 + 4 * f + j, PLANE, stride=CHUNK), :] = filters_ref[f, :, lanes]
    o_ref[...] = scratch[...].astype(bf16)


def outer_forward(signal, first):
    high, low = split(signal)
    return mm(first[0], jnp.concatenate([high, low], axis=0)) + mm(first[1][:, ROWS:], high)


def inner_forward(stages, twiddle, spin, second):
    rows = []
    for stage in stages:
        real, imag = stage[:ROWS], stage[ROWS:]
        turned = (real * twiddle[0] - imag * twiddle[1], real * twiddle[1] + imag * twiddle[0])
        even = [part[:, :HALF] + part[:, HALF:] for part in turned]
        odd = [part[:, :HALF] - part[:, HALF:] for part in turned]
        odd = [odd[0] * spin[0] - odd[1] * spin[1], odd[0] * spin[1] + odd[1] * spin[0]]
        rows += [jnp.concatenate(even, axis=1), jnp.concatenate(odd, axis=1)]
    product = right_product(jnp.concatenate(rows, axis=0), second)
    return [
        (product[2 * ROWS * s : 2 * ROWS * (s + 1), :HALF],
         product[2 * ROWS * s : 2 * ROWS * (s + 1), HALF:])
        for s in range(len(stages))
    ]


def inverse(spectrum, last, twiddle, spin, second):
    product = right_product(jnp.concatenate([spectrum[1], spectrum[0]], axis=1), second)
    even_imag, even_real = product[:ROWS, :HALF], product[:ROWS, HALF:]
    odd_imag, odd_real = product[ROWS:, :HALF], product[ROWS:, HALF:]
    spun_real = odd_real * spin[0] + odd_imag * spin[1]
    spun_imag = odd_imag * spin[0] - odd_real * spin[1]
    real = jnp.concatenate([even_real + spun_real, even_real - spun_real], axis=1)
    imag = jnp.concatenate([even_imag + spun_imag, even_imag - spun_imag], axis=1)
    turned_real = real * twiddle[0] + imag * twiddle[1]
    turned_imag = imag * twiddle[0] - real * twiddle[1]
    return left_product(last, jnp.concatenate([turned_real, turned_imag], axis=0))


def times(left, right):
    return (left[0] * right[0] - left[1] * right[1], left[0] * right[1] + left[1] * right[0])


def short_filter(blocks, taps, group):
    lane = lax.broadcasted_iota(jnp.int32, (PLANE, COLS), 1)
    chip = lax.broadcasted_iota(jnp.int32, (PLANE, COLS), 0)
    shifted = []
    for by in (1, 2):
        rolled = [pltpu.roll(block, by, 1) for block in blocks]
        before = jnp.where(chip == 0, 0.0, pltpu.roll(rolled[3], 1, 0))
        edges = [before, rolled[0], rolled[1], rolled[2]]
        shifted.append([jnp.where(lane < by, edges[q], rolled[q]) for q in range(4)])
    tap = [taps[group : group + 1, j : j + 1] for j in range(3)]
    return [
        tap[0] * blocks[q] + tap[1] * shifted[0][q] + tap[2] * shifted[1][q] for q in range(4)
    ]


def convolve(core, loaded, taps, gains, first, last, own_last, twiddle, spin, second):
    def classes(array):
        return [
            jnp.concatenate([loaded(q // 2, array, 2 * (q % 2) + h) for h in range(2)], axis=1)
            for q in range(4)
        ]

    groups = [jnp.concatenate(short_filter(classes(g), taps, g), axis=0) for g in range(3)]
    responses = jnp.concatenate(
        [jnp.concatenate(classes(3 + f), axis=0).astype(bf16) for f in range(2)], axis=1
    )
    values, first_gate, second_gate = groups
    pair = mm(first[1], jnp.concatenate([responses, responses], axis=0))
    value_spectrum, first_spectrum = inner_forward(
        [outer_forward(values, first), pair[:, :COLS]], twiddle, spin, second
    )
    (second_spectrum,) = inner_forward([pair[:, COLS:]], twiddle, spin, second)
    convolved = inverse(times(value_spectrum, first_spectrum), last, twiddle, spin, second)
    gated = first_gate * (convolved + gains[:, 0:1] * values)
    (gated_spectrum,) = inner_forward([outer_forward(gated, first)], twiddle, spin, second)
    own = inverse(times(gated_spectrum, second_spectrum), own_last, twiddle, spin, second)
    half = ROWS // 2
    own_gated = jnp.where(core == 0, gated[:half], gated[half:])
    own_gate = jnp.where(core == 0, second_gate[:half], second_gate[half:])
    return own_gate * (own + gains[:, 1:2] * own_gated)


def convolve_kernel(
    mine_ref, other_ref, taps_ref, gains_ref, first_ref, last_ref, twiddle_ref, spin_ref,
    second_ref, o_ref, wide, result,
):
    device = lax.axis_index("seq")
    core = device % 2
    channel = device // 2
    half = ROWS // 2
    wide[core] = mine_ref[...].astype(f32)
    wide[1 - core] = other_ref[...].astype(f32)
    mixed = convolve(
        core,
        lambda k, array, j: wide[k, pl.ds(4 * array + j, PLANE, stride=CHUNK), :],
        taps_ref[channel],
        gains_ref[pl.ds(channel, 1), :],
        first_ref,
        last_ref,
        [last_ref[i, pl.ds(pl.multiple_of(half * core, half), half), :] for i in range(2)],
        twiddle_ref,
        spin_ref,
        second_ref,
    )
    for j in range(4):
        result[pl.ds(j, PLANE, stride=4), :] = mixed[
            PLANE * (j // 2) : PLANE * (j // 2 + 1), 128 * (j % 2) : 128 * (j % 2 + 1)
        ]
    out = result[...].astype(bf16)
    for z in range(GROUPS):
        o_ref[z] = out


def output_kernel(r_ref, weights_ref, o_ref, scratch):
    scratch[...] = r_ref[...].astype(f32)
    mixed = jnp.concatenate(
        [scratch[pl.ds(j, 256, stride=4), :].astype(bf16) for j in range(4)], axis=1
    )
    weights = weights_ref[:, BLOCK + 96 : BLOCK + 128]
    o_ref[...] = lax.dot_general(
        weights, mixed, (((0,), (0,)), ((), ())), preferred_element_type=f32
    ).astype(bf16)


def grant(mebibytes):
    return pltpu.CompilerParams(vmem_limit_bytes=mebibytes * 1024 * 1024)


def local(inputs, proj_weight, short_taps, skip_gain, filters, out_weight):
    table = tables()
    hbm = pl.BlockSpec(memory_space=pltpu.HBM)
    packed = pl.pallas_call(
        pack_kernel,
        out_shape=jax.ShapeDtypeStruct((GROUPS, 32, BLOCK + 128), bf16),
        in_specs=[hbm] * 3,
        scratch_shapes=[
            pltpu.VMEM((3, 32, 256), bf16),
            pltpu.VMEM((32, 256), bf16),
            pltpu.SemaphoreType.DMA((GROUPS + 2,)),
        ],
        compiler_params=grant(4),
        name="pack",
    )(*(pltpu.with_memory_space_constraint(a, pltpu.HBM) for a in (inputs, proj_weight, out_weight)))
    gathered = lax.all_to_all(packed, "ch", 0, 0, tiled=True).reshape(256, BLOCK + 128)

    sent = pl.pallas_call(
        project_kernel,
        out_shape=jax.ShapeDtypeStruct((PLANE * CHUNK, 128), bf16),
        scratch_shapes=[pltpu.VMEM((PLANE * CHUNK, 128), f32)],
        compiler_params=grant(8),
        name="project",
    )(gathered, filters)
    same_core = [[2 * c + k for c in range(PLANE)] for k in range(2)]
    mine = lax.all_to_all(
        sent.reshape(PLANE, CHUNK // 4, 4, 128),
        "seq",
        0,
        0,
        tiled=True,
        axis_index_groups=same_core,
    ).reshape(PLANE * CHUNK, 128)
    other = lax.ppermute(mine, "seq", [(i, i ^ 1) for i in range(2 * PLANE)])

    mixed = pl.pallas_call(
        convolve_kernel,
        out_shape=jax.ShapeDtypeStruct((GROUPS, 128, 128), bf16),
        scratch_shapes=[
            pltpu.VMEM((2, PLANE * CHUNK, 128), f32),
            pltpu.VMEM((128, 128), f32),
        ],
        compiler_params=grant(24),
        name="convolve",
    )(
        mine,
        other,
        short_taps,
        skip_gain,
        table["first"],
        table["last"],
        table["twiddle"],
        table["spin"],
        table["second"],
    )
    everyone = [
        [(2 * c + k) * GROUPS + z for z in range(GROUPS) for c in range(PLANE)] for k in range(2)
    ]
    arrived = lax.all_to_all(
        mixed.reshape(256, 4, 128),
        ("seq", "ch"),
        0,
        0,
        tiled=True,
        axis_index_groups=everyone,
    ).reshape(1024, 128)
    return pl.pallas_call(
        output_kernel,
        out_shape=jax.ShapeDtypeStruct((32, BLOCK), bf16),
        scratch_shapes=[pltpu.VMEM((1024, 128), f32)],
        compiler_params=grant(8),
        name="output",
    )(arrived, gathered)


def solution(mesh):
    in_specs = (
        P("ch", "seq"),
        P(None, "ch", None),
        P("ch", None, None),
        P("ch", None),
        P(None, "ch", "seq"),
        P("ch", None),
    )
    return jax.shard_map(
        local, mesh=mesh, in_specs=in_specs, out_specs=P("ch", "seq"), check_vma=False
    )
```

```python
import functools

import jax
import jax.numpy as jnp
import numpy as np
from jax import lax
from jax.experimental import pallas as pl
from jax.experimental.pallas import tpu as pltpu
from jax.sharding import PartitionSpec as P


bf16 = jnp.bfloat16
f32 = jnp.float32

ROWS = 128
COLS = 256
TOTAL = ROWS * COLS
HALF = COLS // 2
PLANE = 32
GROUPS = 8
BLOCK = 512
CHUNK = 20


def split(values):
    high = values.astype(bf16)
    return high, (values - high.astype(f32)).astype(bf16)


def halves(table):
    table = np.asarray(table, np.float32)
    high = table.astype(jnp.bfloat16)
    low = (table - high.astype(np.float32)).astype(jnp.bfloat16)
    return high, low


@functools.cache
def tables():
    row = (4 * np.arange(PLANE)[None, :] + np.arange(4)[:, None]).reshape(-1).astype(np.float64)
    freq = 4.0 * np.arange(ROWS) + 1.0
    angle = 2.0 * np.pi * ((freq[:, None] * row[None, :]) % (4 * ROWS)) / (4 * ROWS)
    first = np.concatenate([np.cos(angle), -np.sin(angle)], axis=0)
    column = np.arange(COLS, dtype=np.float64)
    turn = 2.0 * np.pi * ((freq[:, None] * column[None, :]) % (4 * TOTAL)) / (4 * TOTAL)
    part = column[:HALF]
    inner = 2.0 * np.pi * ((part[:, None] * part[None, :]) % HALF) / HALF
    cosine, sine = np.cos(inner), np.sin(inner)
    spin = 2.0 * np.pi * part[None, :] / COLS
    high, low = halves(first)
    return {
        "first": np.stack(
            [np.concatenate([high, high], axis=1), np.concatenate([high, low], axis=1)]
        ),
        "last": np.stack(halves(first.T / TOTAL)),
        "twiddle": np.stack([np.cos(turn), -np.sin(turn)]).astype(np.float32),
        "spin": np.stack([np.cos(spin), -np.sin(spin)]).astype(np.float32),
        "second": np.stack(halves(np.block([[cosine, -sine], [sine, cosine]]))),
    }


def mm(left, right):
    return jnp.dot(left, right, preferred_element_type=f32)


def left_product(table, values):
    high, low = split(values)
    return mm(table[0], high) + mm(table[0], low) + mm(table[1], high)


def right_product(values, table):
    high, low = split(values)
    return mm(high, table[0]) + mm(low, table[0]) + mm(high, table[1])


def pack_kernel(x_hbm, proj_hbm, out_w_hbm, o_ref, proj_ref, out_w_ref, sems):
    loads = [
        pltpu.make_async_copy(proj_hbm, proj_ref, sems.at[GROUPS]),
        pltpu.make_async_copy(out_w_hbm, out_w_ref, sems.at[GROUPS + 1]),
    ]
    spread = [
        pltpu.make_async_copy(x_hbm, o_ref.at[z, :, pl.ds(0, BLOCK)], sems.at[z])
        for z in range(GROUPS)
    ]
    for copy in loads + spread:
        copy.start()
    for copy in loads:
        copy.wait()
    weights = [proj_ref[g].astype(f32) for g in range(3)] + [out_w_ref[...].astype(f32)]
    lane = lax.broadcasted_iota(jnp.int32, (32, 128), 1) // 32
    for z in range(GROUPS):
        tile, offset = z // 4, z % 4
        picked = None
        for g in range(4):
            piece = weights[g][:, 128 * tile : 128 * tile + 128]
            by = (32 * (g - offset)) % 128
            if by:
                piece = pltpu.roll(piece, by, 1)
            picked = piece if picked is None else jnp.where(lane == g, piece, picked)
        o_ref[z, :, BLOCK : BLOCK + 128] = picked.astype(bf16)
    for copy in spread:
        copy.wait()


def project_kernel(r_ref, filters_ref, o_ref, scratch):
    x = r_ref[:, 0:BLOCK]
    weights = r_ref[:, BLOCK : BLOCK + 128]
    projected = lax.dot_general(
        weights, x, (((0,), (0,)), ((), ())), preferred_element_type=f32
    )
    for j in range(4):
        lanes = slice(128 * j, 128 * (j + 1))
        for g in range(3):
            scratch[pl.ds(4 * g + j, PLANE, stride=CHUNK), :] = projected[
                PLANE * g : PLANE * (g + 1), lanes
            ]
        for f in range(2):
            scratch[pl.ds(12 + 4 * f + j, PLANE, stride=CHUNK), :] = filters_ref[f, :, lanes]
    o_ref[...] = scratch[...].astype(bf16)


def outer_forward(signal, first):
    high, low = split(signal)
    return mm(first[0], jnp.concatenate([high, low], axis=0)) + mm(first[1][:, ROWS:], high)


def inner_forward(stages, twiddle, spin, second):
    rows = []
    for stage in stages:
        real, imag = stage[:ROWS], stage[ROWS:]
        turned = (real * twiddle[0] - imag * twiddle[1], real * twiddle[1] + imag * twiddle[0])
        even = [part[:, :HALF] + part[:, HALF:] for part in turned]
        odd = [part[:, :HALF] - part[:, HALF:] for part in turned]
        odd = [odd[0] * spin[0] - odd[1] * spin[1], odd[0] * spin[1] + odd[1] * spin[0]]
        rows += [jnp.concatenate(even, axis=1), jnp.concatenate(odd, axis=1)]
    product = right_product(jnp.concatenate(rows, axis=0), second)
    return [
        (product[2 * ROWS * s : 2 * ROWS * (s + 1), :HALF],
         product[2 * ROWS * s : 2 * ROWS * (s + 1), HALF:])
        for s in range(len(stages))
    ]


def inverse(spectrum, last, twiddle, spin, second):
    product = right_product(jnp.concatenate([spectrum[1], spectrum[0]], axis=1), second)
    even_imag, even_real = product[:ROWS, :HALF], product[:ROWS, HALF:]
    odd_imag, odd_real = product[ROWS:, :HALF], product[ROWS:, HALF:]
    spun_real = odd_real * spin[0] + odd_imag * spin[1]
    spun_imag = odd_imag * spin[0] - odd_real * spin[1]
    real = jnp.concatenate([even_real + spun_real, even_real - spun_real], axis=1)
    imag = jnp.concatenate([even_imag + spun_imag, even_imag - spun_imag], axis=1)
    turned_real = real * twiddle[0] + imag * twiddle[1]
    turned_imag = imag * twiddle[0] - real * twiddle[1]
    return left_product(last, jnp.concatenate([turned_real, turned_imag], axis=0))


def times(left, right):
    return (left[0] * right[0] - left[1] * right[1], left[0] * right[1] + left[1] * right[0])


def short_filter(blocks, taps, group):
    lane = lax.broadcasted_iota(jnp.int32, (PLANE, COLS), 1)
    chip = lax.broadcasted_iota(jnp.int32, (PLANE, COLS), 0)
    shifted = []
    for by in (1, 2):
        rolled = [pltpu.roll(block, by, 1) for block in blocks]
        before = jnp.where(chip == 0, 0.0, pltpu.roll(rolled[3], 1, 0))
        edges = [before, rolled[0], rolled[1], rolled[2]]
        shifted.append([jnp.where(lane < by, edges[q], rolled[q]) for q in range(4)])
    tap = [taps[group : group + 1, j : j + 1] for j in range(3)]
    return [
        tap[0] * blocks[q] + tap[1] * shifted[0][q] + tap[2] * shifted[1][q] for q in range(4)
    ]


def convolve(core, loaded, taps, gains, first, last, own_last, twiddle, spin, second):
    def classes(array):
        return [
            jnp.concatenate([loaded(q // 2, array, 2 * (q % 2) + h) for h in range(2)], axis=1)
            for q in range(4)
        ]

    groups = [jnp.concatenate(short_filter(classes(g), taps, g), axis=0) for g in range(3)]
    responses = jnp.concatenate(
        [jnp.concatenate(classes(3 + f), axis=0).astype(bf16) for f in range(2)], axis=1
    )
    values, first_gate, second_gate = groups
    pair = mm(first[1], jnp.concatenate([responses, responses], axis=0))
    value_spectrum, first_spectrum = inner_forward(
        [outer_forward(values, first), pair[:, :COLS]], twiddle, spin, second
    )
    (second_spectrum,) = inner_forward([pair[:, COLS:]], twiddle, spin, second)
    convolved = inverse(times(value_spectrum, first_spectrum), last, twiddle, spin, second)
    gated = first_gate * (convolved + gains[:, 0:1] * values)
    (gated_spectrum,) = inner_forward([outer_forward(gated, first)], twiddle, spin, second)
    own = inverse(times(gated_spectrum, second_spectrum), own_last, twiddle, spin, second)
    half = ROWS // 2
    own_gated = jnp.where(core == 0, gated[:half], gated[half:])
    own_gate = jnp.where(core == 0, second_gate[:half], second_gate[half:])
    return own_gate * (own + gains[:, 1:2] * own_gated)


def convolve_kernel(
    mine_ref, other_ref, taps_ref, gains_ref, first_ref, last_ref, twiddle_ref, spin_ref,
    second_ref, o_ref, wide, result,
):
    device = lax.axis_index("seq")
    core = device % 2
    channel = device // 2
    half = ROWS // 2
    wide[core] = mine_ref[...].astype(f32)
    wide[1 - core] = other_ref[...].astype(f32)
    mixed = convolve(
        core,
        lambda k, array, j: wide[k, pl.ds(4 * array + j, PLANE, stride=CHUNK), :],
        taps_ref[channel],
        gains_ref[pl.ds(channel, 1), :],
        first_ref,
        last_ref,
        [last_ref[i, pl.ds(pl.multiple_of(half * core, half), half), :] for i in range(2)],
        twiddle_ref,
        spin_ref,
        second_ref,
    )
    for j in range(4):
        result[pl.ds(j, PLANE, stride=4), :] = mixed[
            PLANE * (j // 2) : PLANE * (j // 2 + 1), 128 * (j % 2) : 128 * (j % 2 + 1)
        ]
    out = result[...].astype(bf16)
    for z in range(GROUPS):
        o_ref[z] = out


def output_kernel(r_ref, weights_ref, o_ref, scratch):
    scratch[...] = r_ref[...].astype(f32)
    mixed = jnp.concatenate(
        [scratch[pl.ds(j, 256, stride=4), :].astype(bf16) for j in range(4)], axis=1
    )
    o_ref[...] = mm(weights_ref[...], mixed).astype(bf16)


def turn_kernel(r_ref, o_ref):
    weights = r_ref[:, BLOCK : BLOCK + 128].astype(f32)
    o_ref[...] = weights.T[96:128].astype(bf16)


def grant(mebibytes):
    return pltpu.CompilerParams(vmem_limit_bytes=mebibytes * 1024 * 1024)


def local(inputs, proj_weight, short_taps, skip_gain, filters, out_weight):
    table = tables()
    hbm = pl.BlockSpec(memory_space=pltpu.HBM)
    packed = pl.pallas_call(
        pack_kernel,
        out_shape=jax.ShapeDtypeStruct((GROUPS, 32, BLOCK + 128), bf16),
        in_specs=[hbm] * 3,
        scratch_shapes=[
            pltpu.VMEM((3, 32, 256), bf16),
            pltpu.VMEM((32, 256), bf16),
            pltpu.SemaphoreType.DMA((GROUPS + 2,)),
        ],
        compiler_params=grant(4),
        name="pack",
    )(*(pltpu.with_memory_space_constraint(a, pltpu.HBM) for a in (inputs, proj_weight, out_weight)))
    gathered = lax.all_to_all(packed, "ch", 0, 0, tiled=True).reshape(256, BLOCK + 128)

    sent = pl.pallas_call(
        project_kernel,
        out_shape=jax.ShapeDtypeStruct((PLANE * CHUNK, 128), bf16),
        scratch_shapes=[pltpu.VMEM((PLANE * CHUNK, 128), f32)],
        compiler_params=grant(8),
        name="project",
    )(gathered, filters)
    same_core = [[2 * c + k for c in range(PLANE)] for k in range(2)]
    mine = lax.all_to_all(
        sent.reshape(PLANE, CHUNK // 4, 4, 128),
        "seq",
        0,
        0,
        tiled=True,
        axis_index_groups=same_core,
    ).reshape(PLANE * CHUNK, 128)
    other = lax.ppermute(mine, "seq", [(i, i ^ 1) for i in range(2 * PLANE)])

    mixed = pl.pallas_call(
        convolve_kernel,
        out_shape=jax.ShapeDtypeStruct((GROUPS, 128, 128), bf16),
        scratch_shapes=[
            pltpu.VMEM((2, PLANE * CHUNK, 128), f32),
            pltpu.VMEM((128, 128), f32),
        ],
        compiler_params=grant(24),
        name="convolve",
    )(
        mine,
        other,
        short_taps,
        skip_gain,
        table["first"],
        table["last"],
        table["twiddle"],
        table["spin"],
        table["second"],
    )
    everyone = [
        [(2 * c + k) * GROUPS + z for z in range(GROUPS) for c in range(PLANE)] for k in range(2)
    ]
    arrived = lax.all_to_all(
        mixed.reshape(256, 4, 128),
        ("seq", "ch"),
        0,
        0,
        tiled=True,
        axis_index_groups=everyone,
    )
    turned = pl.pallas_call(
        turn_kernel,
        out_shape=jax.ShapeDtypeStruct((32, 256), bf16),
        compiler_params=grant(4),
        cost_estimate=pl.CostEstimate(flops=1000000, bytes_accessed=1000000, transcendentals=0),
        name="turn",
    )(gathered)
    return pl.pallas_call(
        output_kernel,
        out_shape=jax.ShapeDtypeStruct((32, BLOCK), bf16),
        scratch_shapes=[pltpu.VMEM((1024, 128), f32)],
        compiler_params=grant(8),
        name="output",
    )(arrived.reshape(1024, 128), turned)


def solution(mesh):
    in_specs = (
        P("ch", "seq"),
        P(None, "ch", None),
        P("ch", None, None),
        P("ch", None),
        P(None, "ch", "seq"),
        P("ch", None),
    )
    return jax.shard_map(
        local, mesh=mesh, in_specs=in_specs, out_specs=P("ch", "seq"), check_vma=False
    )
```

```python
import functools

import jax
import jax.numpy as jnp
import numpy as np
from jax import lax
from jax.experimental import pallas as pl
from jax.experimental.pallas import tpu as pltpu
from jax.sharding import PartitionSpec as P

bf16 = jnp.bfloat16
f32 = jnp.float32

ROWS = 128
COLS = 256
TOTAL = ROWS * COLS
HALF = COLS // 2
PLANE = 32
GROUPS = 8
BLOCK = 512
CHUNK = 20


def split(values):
    high = values.astype(bf16)
    return high, (values - high.astype(f32)).astype(bf16)


def halves(table):
    table = np.asarray(table, np.float32)
    high = table.astype(jnp.bfloat16)
    low = (table - high.astype(np.float32)).astype(jnp.bfloat16)
    return high, low


@functools.cache
def tables():
    row = (4 * np.arange(PLANE)[None, :] + np.arange(4)[:, None]).reshape(-1).astype(np.float64)
    freq = 4.0 * np.arange(ROWS) + 1.0
    angle = 2.0 * np.pi * ((freq[:, None] * row[None, :]) % (4 * ROWS)) / (4 * ROWS)
    first = np.concatenate([np.cos(angle), -np.sin(angle)], axis=0)
    column = np.arange(COLS, dtype=np.float64)
    turn = 2.0 * np.pi * ((freq[:, None] * column[None, :]) % (4 * TOTAL)) / (4 * TOTAL)
    part = column[:HALF]
    inner = 2.0 * np.pi * ((part[:, None] * part[None, :]) % HALF) / HALF
    cosine, sine = np.cos(inner), np.sin(inner)
    spin = 2.0 * np.pi * part[None, :] / COLS
    high, low = halves(first)
    return {
        "first": np.stack(
            [np.concatenate([high, high], axis=1), np.concatenate([high, low], axis=1)]
        ),
        "last": np.stack(halves(first.T / TOTAL)),
        "twiddle": np.stack([np.cos(turn), -np.sin(turn)]).astype(np.float32),
        "spin": np.stack([np.cos(spin), -np.sin(spin)]).astype(np.float32),
        "second": np.stack(halves(np.block([[cosine, -sine], [sine, cosine]]))),
    }


def mm(left, right):
    return jnp.dot(left, right, preferred_element_type=f32)


def left_product(table, values):
    high, low = split(values)
    return mm(table[0], high) + mm(table[0], low) + mm(table[1], high)


def right_product(values, table):
    parts = []
    for at in range(0, values.shape[0], 128):
        high, low = split(values[at : at + 128])
        parts.append(mm(high, table[0]) + mm(low, table[0]) + mm(high, table[1]))
    return jnp.concatenate(parts, axis=0)


def pack_kernel(x_hbm, proj_hbm, out_w_hbm, o_ref, proj_ref, out_w_ref, sems):
    loads = [
        pltpu.make_async_copy(proj_hbm, proj_ref, sems.at[GROUPS]),
        pltpu.make_async_copy(out_w_hbm, out_w_ref, sems.at[GROUPS + 1]),
    ]
    spread = [
        pltpu.make_async_copy(x_hbm, o_ref.at[z, :, pl.ds(0, BLOCK)], sems.at[z])
        for z in range(GROUPS)
    ]
    for copy in loads + spread:
        copy.start()
    for copy in loads:
        copy.wait()
    weights = [proj_ref[g].astype(f32) for g in range(3)] + [out_w_ref[...].astype(f32)]
    lane = lax.broadcasted_iota(jnp.int32, (32, 128), 1) // 32
    for z in range(GROUPS):
        tile, offset = z // 4, z % 4
        picked = None
        for g in range(4):
            piece = weights[g][:, 128 * tile : 128 * tile + 128]
            by = (32 * (g - offset)) % 128
            if by:
                piece = pltpu.roll(piece, by, 1)
            picked = piece if picked is None else jnp.where(lane == g, piece, picked)
        o_ref[z, :, BLOCK : BLOCK + 128] = picked.astype(bf16)
    for copy in spread:
        copy.wait()


def project_kernel(r_ref, filters_ref, o_ref, scratch):
    x = r_ref[:, 0:BLOCK]
    weights = r_ref[:, BLOCK : BLOCK + 128]
    projected = lax.dot_general(
        weights, x, (((0,), (0,)), ((), ())), preferred_element_type=f32
    )
    for j in range(4):
        lanes = slice(128 * j, 128 * (j + 1))
        for g in range(3):
            scratch[pl.ds(4 * g + j, PLANE, stride=CHUNK), :] = projected[
                PLANE * g : PLANE * (g + 1), lanes
            ]
        for f in range(2):
            scratch[pl.ds(12 + 4 * f + j, PLANE, stride=CHUNK), :] = filters_ref[f, :, lanes]
    o_ref[...] = scratch[...].astype(bf16)


def outer_forward(signal, first):
    high, low = split(signal)
    return mm(first[0], jnp.concatenate([high, low], axis=0)) + mm(first[1][:, ROWS:], high)


def inner_forward(stages, twiddle, spin, second):
    rows = []
    for stage in stages:
        real, imag = stage[:ROWS], stage[ROWS:]
        turned = (real * twiddle[0] - imag * twiddle[1], real * twiddle[1] + imag * twiddle[0])
        even = [part[:, :HALF] + part[:, HALF:] for part in turned]
        odd = [part[:, :HALF] - part[:, HALF:] for part in turned]
        odd = [odd[0] * spin[0] - odd[1] * spin[1], odd[0] * spin[1] + odd[1] * spin[0]]
        rows += [jnp.concatenate(even, axis=1), jnp.concatenate(odd, axis=1)]
    product = right_product(jnp.concatenate(rows, axis=0), second)
    return [
        (product[2 * ROWS * s : 2 * ROWS * (s + 1), :HALF],
         product[2 * ROWS * s : 2 * ROWS * (s + 1), HALF:])
        for s in range(len(stages))
    ]


def inverse(spectrum, last, twiddle, spin, second):
    product = right_product(jnp.concatenate([spectrum[1], spectrum[0]], axis=1), second)
    even_imag, even_real = product[:ROWS, :HALF], product[:ROWS, HALF:]
    odd_imag, odd_real = product[ROWS:, :HALF], product[ROWS:, HALF:]
    spun_real = odd_real * spin[0] + odd_imag * spin[1]
    spun_imag = odd_imag * spin[0] - odd_real * spin[1]
    real = jnp.concatenate([even_real + spun_real, even_real - spun_real], axis=1)
    imag = jnp.concatenate([even_imag + spun_imag, even_imag - spun_imag], axis=1)
    turned_real = real * twiddle[0] + imag * twiddle[1]
    turned_imag = imag * twiddle[0] - real * twiddle[1]
    return left_product(last, jnp.concatenate([turned_real, turned_imag], axis=0))


def times(left, right):
    return (left[0] * right[0] - left[1] * right[1], left[0] * right[1] + left[1] * right[0])


def short_filter(blocks, taps, group):
    lane = lax.broadcasted_iota(jnp.int32, (PLANE, COLS), 1)
    chip = lax.broadcasted_iota(jnp.int32, (PLANE, COLS), 0)
    shifted = []
    for by in (1, 2):
        rolled = [pltpu.roll(block, by, 1) for block in blocks]
        before = jnp.where(chip == 0, 0.0, pltpu.roll(rolled[3], 1, 0))
        edges = [before, rolled[0], rolled[1], rolled[2]]
        shifted.append([jnp.where(lane < by, edges[q], rolled[q]) for q in range(4)])
    tap = [taps[group : group + 1, j : j + 1] for j in range(3)]
    return [
        tap[0] * blocks[q] + tap[1] * shifted[0][q] + tap[2] * shifted[1][q] for q in range(4)
    ]


def convolve(core, loaded, taps, gains, first, last, own_last, twiddle, spin, second):
    def classes(array):
        return [
            jnp.concatenate([loaded(q // 2, array, 2 * (q % 2) + h) for h in range(2)], axis=1)
            for q in range(4)
        ]

    groups = [jnp.concatenate(short_filter(classes(g), taps, g), axis=0) for g in range(3)]
    responses = jnp.concatenate(
        [jnp.concatenate(classes(3 + f), axis=0).astype(bf16) for f in range(2)], axis=1
    )
    values, first_gate, second_gate = groups
    pair = mm(first[1], jnp.concatenate([responses, responses], axis=0))
    value_spectrum, first_spectrum = inner_forward(
        [outer_forward(values, first), pair[:, :COLS]], twiddle, spin, second
    )
    (second_spectrum,) = inner_forward([pair[:, COLS:]], twiddle, spin, second)
    convolved = inverse(times(value_spectrum, first_spectrum), last, twiddle, spin, second)
    gated = first_gate * (convolved + gains[:, 0:1] * values)
    (gated_spectrum,) = inner_forward([outer_forward(gated, first)], twiddle, spin, second)
    own = inverse(times(gated_spectrum, second_spectrum), own_last, twiddle, spin, second)
    half = ROWS // 2
    own_gated = jnp.where(core == 0, gated[:half], gated[half:])
    own_gate = jnp.where(core == 0, second_gate[:half], second_gate[half:])
    return own_gate * (own + gains[:, 1:2] * own_gated)


def convolve_kernel(
    mine_ref, other_ref, taps_ref, gains_ref, first_ref, last_ref, twiddle_ref, spin_ref,
    second_ref, o_ref, wide, result,
):
    device = lax.axis_index("seq")
    core = device % 2
    channel = device // 2
    half = ROWS // 2
    wide[core] = mine_ref[...].astype(f32)
    wide[1 - core] = other_ref[...].astype(f32)
    mixed = convolve(
        core,
        lambda k, array, j: wide[k, pl.ds(4 * array + j, PLANE, stride=CHUNK), :],
        taps_ref[channel],
        gains_ref[pl.ds(channel, 1), :],
        first_ref,
        last_ref,
        [last_ref[i, pl.ds(pl.multiple_of(half * core, half), half), :] for i in range(2)],
        twiddle_ref,
        spin_ref,
        second_ref,
    )
    for j in range(4):
        result[pl.ds(j, PLANE, stride=4), :] = mixed[
            PLANE * (j // 2) : PLANE * (j // 2 + 1), 128 * (j % 2) : 128 * (j % 2 + 1)
        ]
    out = result[...].astype(bf16)
    for z in range(GROUPS):
        o_ref[z] = out


def output_kernel(r_ref, weights_ref, o_ref, scratch):
    scratch[...] = r_ref[...].astype(f32)
    mixed = jnp.concatenate(
        [scratch[pl.ds(j, 256, stride=4), :].astype(bf16) for j in range(4)], axis=1
    )
    weights = weights_ref[:, BLOCK + 96 : BLOCK + 128]
    o_ref[...] = lax.dot_general(
        weights, mixed, (((0,), (0,)), ((), ())), preferred_element_type=f32
    ).astype(bf16)


def grant(mebibytes):
    return pltpu.CompilerParams(vmem_limit_bytes=mebibytes * 1024 * 1024)


def local(inputs, proj_weight, short_taps, skip_gain, filters, out_weight):
    table = tables()
    hbm = pl.BlockSpec(memory_space=pltpu.HBM)
    packed = pl.pallas_call(
        pack_kernel,
        out_shape=jax.ShapeDtypeStruct((GROUPS, 32, BLOCK + 128), bf16),
        in_specs=[hbm] * 3,
        scratch_shapes=[
            pltpu.VMEM((3, 32, 256), bf16),
            pltpu.VMEM((32, 256), bf16),
            pltpu.SemaphoreType.DMA((GROUPS + 2,)),
        ],
        compiler_params=grant(4),
        name="pack",
    )(*(pltpu.with_memory_space_constraint(a, pltpu.HBM) for a in (inputs, proj_weight, out_weight)))
    gathered = lax.all_to_all(packed, "ch", 0, 0, tiled=True).reshape(256, BLOCK + 128)

    sent = pl.pallas_call(
        project_kernel,
        out_shape=jax.ShapeDtypeStruct((PLANE * CHUNK, 128), bf16),
        scratch_shapes=[pltpu.VMEM((PLANE * CHUNK, 128), f32)],
        compiler_params=grant(8),
        name="project",
    )(gathered, filters)
    same_core = [[2 * c + k for c in range(PLANE)] for k in range(2)]
    mine = lax.all_to_all(
        sent.reshape(PLANE, CHUNK // 4, 4, 128),
        "seq",
        0,
        0,
        tiled=True,
        axis_index_groups=same_core,
    ).reshape(PLANE * CHUNK, 128)
    other = lax.ppermute(mine, "seq", [(i, i ^ 1) for i in range(2 * PLANE)])

    mixed = pl.pallas_call(
        convolve_kernel,
        out_shape=jax.ShapeDtypeStruct((GROUPS, 128, 128), bf16),
        scratch_shapes=[
            pltpu.VMEM((2, PLANE * CHUNK, 128), f32),
            pltpu.VMEM((128, 128), f32),
        ],
        compiler_params=grant(24),
        name="convolve",
    )(
        mine,
        other,
        short_taps,
        skip_gain,
        table["first"],
        table["last"],
        table["twiddle"],
        table["spin"],
        table["second"],
    )
    everyone = [
        [(2 * c + k) * GROUPS + z for z in range(GROUPS) for c in range(PLANE)] for k in range(2)
    ]
    arrived = lax.all_to_all(
        mixed.reshape(256, 4, 128),
        ("seq", "ch"),
        0,
        0,
        tiled=True,
        axis_index_groups=everyone,
    ).reshape(1024, 128)
    return pl.pallas_call(
        output_kernel,
        out_shape=jax.ShapeDtypeStruct((32, BLOCK), bf16),
        scratch_shapes=[pltpu.VMEM((1024, 128), f32)],
        compiler_params=grant(8),
        name="output",
    )(arrived, gathered)


def solution(mesh):
    in_specs = (
        P("ch", "seq"),
        P(None, "ch", None),
        P("ch", None, None),
        P("ch", None),
        P(None, "ch", "seq"),
        P("ch", None),
    )
    return jax.shard_map(
        local, mesh=mesh, in_specs=in_specs, out_specs=P("ch", "seq"), check_vma=False
    )
```

```python
import functools

import jax
import jax.numpy as jnp
import numpy as np
from jax import lax
from jax.experimental import pallas as pl
from jax.experimental.pallas import tpu as pltpu
from jax.sharding import PartitionSpec as P

bf16 = jnp.bfloat16
f32 = jnp.float32

ROWS = 128
COLS = 256
TOTAL = ROWS * COLS
HALF = COLS // 2
PLANE = 32
GROUPS = 8
BLOCK = 512
CHUNK = 20


def split(values):
    high = values.astype(bf16)
    return high, (values - high.astype(f32)).astype(bf16)


def halves(table):
    table = np.asarray(table, np.float32)
    high = table.astype(jnp.bfloat16)
    low = (table - high.astype(np.float32)).astype(jnp.bfloat16)
    return high, low


@functools.cache
def tables():
    row = (4 * np.arange(PLANE)[None, :] + np.arange(4)[:, None]).reshape(-1).astype(np.float64)
    freq = 4.0 * np.arange(ROWS) + 1.0
    angle = 2.0 * np.pi * ((freq[:, None] * row[None, :]) % (4 * ROWS)) / (4 * ROWS)
    first = np.concatenate([np.cos(angle), -np.sin(angle)], axis=0)
    column = np.arange(COLS, dtype=np.float64)
    turn = 2.0 * np.pi * ((freq[:, None] * column[None, :]) % (4 * TOTAL)) / (4 * TOTAL)
    part = column[:HALF]
    inner = 2.0 * np.pi * ((part[:, None] * part[None, :]) % HALF) / HALF
    cosine, sine = np.cos(inner), np.sin(inner)
    spin = 2.0 * np.pi * part[None, :] / COLS
    high, low = halves(first)
    return {
        "first": np.stack(
            [np.concatenate([high, high], axis=1), np.concatenate([high, low], axis=1)]
        ),
        "last": np.stack(halves(first.T / TOTAL)),
        "twiddle": np.stack([np.cos(turn), -np.sin(turn)]).astype(np.float32),
        "spin": np.stack([np.cos(spin), -np.sin(spin)]).astype(np.float32),
        "second": np.stack(halves(np.block([[cosine, -sine], [sine, cosine]]))),
    }


def mm(left, right):
    return jnp.dot(left, right, preferred_element_type=f32)


def left_product(table, values):
    high, low = split(values)
    return mm(table[0], high) + mm(table[0], low) + mm(table[1], high)


def right_product(values, table):
    parts = []
    for at in range(0, values.shape[0], 128):
        high, low = split(values[at : at + 128])
        parts.append(mm(high, table[0]) + mm(low, table[0]) + mm(high, table[1]))
    return jnp.concatenate(parts, axis=0)


def pack_kernel(x_hbm, proj_hbm, out_w_hbm, o_ref, proj_ref, out_w_ref, sems):
    loads = [
        pltpu.make_async_copy(proj_hbm, proj_ref, sems.at[GROUPS]),
        pltpu.make_async_copy(out_w_hbm, out_w_ref, sems.at[GROUPS + 1]),
    ]
    spread = [
        pltpu.make_async_copy(x_hbm, o_ref.at[z, :, pl.ds(0, BLOCK)], sems.at[z])
        for z in range(GROUPS)
    ]
    for copy in loads + spread:
        copy.start()
    for copy in loads:
        copy.wait()
    weights = [proj_ref[g].astype(f32) for g in range(3)] + [out_w_ref[...].astype(f32)]
    lane = lax.broadcasted_iota(jnp.int32, (32, 128), 1) // 32
    for z in range(GROUPS):
        tile, offset = z // 4, z % 4
        picked = None
        for g in range(4):
            piece = weights[g][:, 128 * tile : 128 * tile + 128]
            by = (32 * (g - offset)) % 128
            if by:
                piece = pltpu.roll(piece, by, 1)
            picked = piece if picked is None else jnp.where(lane == g, piece, picked)
        o_ref[z, :, BLOCK : BLOCK + 128] = picked.astype(bf16)
    for copy in spread:
        copy.wait()


def project_kernel(r_ref, filters_ref, o_ref, out_w_ref, scratch):
    weights = r_ref[:, BLOCK : BLOCK + 128].astype(f32).T.astype(bf16)
    out_w_ref[...] = weights[96:128]
    projected = mm(weights[0:96], r_ref[:, 0:BLOCK])
    for j in range(4):
        lanes = slice(128 * j, 128 * (j + 1))
        for g in range(3):
            scratch[pl.ds(4 * g + j, PLANE, stride=CHUNK), :] = projected[
                PLANE * g : PLANE * (g + 1), lanes
            ]
        for f in range(2):
            scratch[pl.ds(12 + 4 * f + j, PLANE, stride=CHUNK), :] = filters_ref[f, :, lanes]
    o_ref[...] = scratch[...].astype(bf16)


def outer_forward(signal, first):
    high, low = split(signal)
    return mm(first[0], jnp.concatenate([high, low], axis=0)) + mm(first[1][:, ROWS:], high)


def inner_forward(stages, twiddle, spin, second):
    rows = []
    for stage in stages:
        real, imag = stage[:ROWS], stage[ROWS:]
        turned = (real * twiddle[0] - imag * twiddle[1], real * twiddle[1] + imag * twiddle[0])
        even = [part[:, :HALF] + part[:, HALF:] for part in turned]
        odd = [part[:, :HALF] - part[:, HALF:] for part in turned]
        odd = [odd[0] * spin[0] - odd[1] * spin[1], odd[0] * spin[1] + odd[1] * spin[0]]
        rows += [jnp.concatenate(even, axis=1), jnp.concatenate(odd, axis=1)]
    product = right_product(jnp.concatenate(rows, axis=0), second)
    return [
        (product[2 * ROWS * s : 2 * ROWS * (s + 1), :HALF],
         product[2 * ROWS * s : 2 * ROWS * (s + 1), HALF:])
        for s in range(len(stages))
    ]


def inverse(spectrum, last, twiddle, spin, second):
    product = right_product(jnp.concatenate([spectrum[1], spectrum[0]], axis=1), second)
    even_imag, even_real = product[:ROWS, :HALF], product[:ROWS, HALF:]
    odd_imag, odd_real = product[ROWS:, :HALF], product[ROWS:, HALF:]
    spun_real = odd_real * spin[0] + odd_imag * spin[1]
    spun_imag = odd_imag * spin[0] - odd_real * spin[1]
    real = jnp.concatenate([even_real + spun_real, even_real - spun_real], axis=1)
    imag = jnp.concatenate([even_imag + spun_imag, even_imag - spun_imag], axis=1)
    turned_real = real * twiddle[0] + imag * twiddle[1]
    turned_imag = imag * twiddle[0] - real * twiddle[1]
    return left_product(last, jnp.concatenate([turned_real, turned_imag], axis=0))


def times(left, right):
    return (left[0] * right[0] - left[1] * right[1], left[0] * right[1] + left[1] * right[0])


def short_filter(blocks, taps, group):
    lane = lax.broadcasted_iota(jnp.int32, (PLANE, COLS), 1)
    chip = lax.broadcasted_iota(jnp.int32, (PLANE, COLS), 0)
    shifted = []
    for by in (1, 2):
        rolled = [pltpu.roll(block, by, 1) for block in blocks]
        before = jnp.where(chip == 0, 0.0, pltpu.roll(rolled[3], 1, 0))
        edges = [before, rolled[0], rolled[1], rolled[2]]
        shifted.append([jnp.where(lane < by, edges[q], rolled[q]) for q in range(4)])
    tap = [taps[group : group + 1, j : j + 1] for j in range(3)]
    return [
        tap[0] * blocks[q] + tap[1] * shifted[0][q] + tap[2] * shifted[1][q] for q in range(4)
    ]


def convolve(core, loaded, taps, gains, first, last, own_last, twiddle, spin, second):
    def classes(array):
        return [
            jnp.concatenate([loaded(q // 2, array, 2 * (q % 2) + h) for h in range(2)], axis=1)
            for q in range(4)
        ]

    values, first_gate = [
        jnp.concatenate(short_filter(classes(g), taps, g), axis=0) for g in range(2)
    ]
    responses = jnp.concatenate(
        [jnp.concatenate(classes(3 + f), axis=0).astype(bf16) for f in range(2)], axis=1
    )
    pair = mm(first[1], jnp.concatenate([responses, responses], axis=0))
    value_spectrum, first_spectrum = inner_forward(
        [outer_forward(values, first), pair[:, :COLS]], twiddle, spin, second
    )
    (second_spectrum,) = inner_forward([pair[:, COLS:]], twiddle, spin, second)
    convolved = inverse(times(value_spectrum, first_spectrum), last, twiddle, spin, second)
    gated = first_gate * (convolved + gains[:, 0:1] * values)
    (gated_spectrum,) = inner_forward([outer_forward(gated, first)], twiddle, spin, second)
    own = inverse(times(gated_spectrum, second_spectrum), own_last, twiddle, spin, second)
    half = ROWS // 2
    own_gated = jnp.where(core == 0, gated[:half], gated[half:])
    lane = lax.broadcasted_iota(jnp.int32, (PLANE, COLS), 1)
    chip = lax.broadcasted_iota(jnp.int32, (PLANE, COLS), 0)
    near = [
        jnp.concatenate([loaded(core, 2, 2 * r + h) for h in range(2)], axis=1) for r in range(2)
    ]
    far = jnp.concatenate([loaded(1 - core, 2, 2 + h) for h in range(2)], axis=1)
    tap = [taps[2:3, j : j + 1] for j in range(3)]
    own_gate = [tap[0] * near[0], tap[0] * near[1]]
    for by in (1, 2):
        edge = pltpu.roll(far, by, 1)
        down = jnp.where(chip == 0, 0.0, pltpu.roll(edge, 1, 0))
        edge = jnp.where(core == 0, down, edge)
        rolled = [pltpu.roll(part, by, 1) for part in near]
        own_gate[0] += tap[by] * jnp.where(lane < by, edge, rolled[0])
        own_gate[1] += tap[by] * jnp.where(lane < by, rolled[0], rolled[1])
    own_gate = jnp.concatenate(own_gate, axis=0)
    return own_gate * (own + gains[:, 1:2] * own_gated)


def convolve_kernel(
    mine_ref, other_ref, taps_ref, gains_ref, first_ref, last_ref, twiddle_ref, spin_ref,
    second_ref, o_ref, wide, result,
):
    device = lax.axis_index("seq")
    core = device % 2
    channel = device // 2
    half = ROWS // 2
    wide[core] = mine_ref[...].astype(f32)
    wide[1 - core] = other_ref[...].astype(f32)
    mixed = convolve(
        core,
        lambda k, array, j: wide[k, pl.ds(4 * array + j, PLANE, stride=CHUNK), :],
        taps_ref[channel],
        gains_ref[pl.ds(channel, 1), :],
        first_ref,
        last_ref,
        [last_ref[i, pl.ds(pl.multiple_of(half * core, half), half), :] for i in range(2)],
        twiddle_ref,
        spin_ref,
        second_ref,
    )
    for j in range(4):
        result[pl.ds(j, PLANE, stride=4), :] = mixed[
            PLANE * (j // 2) : PLANE * (j // 2 + 1), 128 * (j % 2) : 128 * (j % 2 + 1)
        ]
    out = result[...].astype(bf16)
    for z in range(GROUPS):
        o_ref[z] = out


def output_kernel(r_ref, weights_ref, o_ref, scratch):
    scratch[...] = r_ref[...].astype(f32)
    mixed = jnp.concatenate(
        [scratch[pl.ds(j, 256, stride=4), :].astype(bf16) for j in range(4)], axis=1
    )
    o_ref[...] = mm(weights_ref[...], mixed).astype(bf16)


def grant(mebibytes):
    return pltpu.CompilerParams(vmem_limit_bytes=mebibytes * 1024 * 1024)


def local(inputs, proj_weight, short_taps, skip_gain, filters, out_weight):
    table = tables()
    hbm = pl.BlockSpec(memory_space=pltpu.HBM)
    packed = pl.pallas_call(
        pack_kernel,
        out_shape=jax.ShapeDtypeStruct((GROUPS, 32, BLOCK + 128), bf16),
        in_specs=[hbm] * 3,
        scratch_shapes=[
            pltpu.VMEM((3, 32, 256), bf16),
            pltpu.VMEM((32, 256), bf16),
            pltpu.SemaphoreType.DMA((GROUPS + 2,)),
        ],
        compiler_params=grant(4),
        name="pack",
    )(*(pltpu.with_memory_space_constraint(a, pltpu.HBM) for a in (inputs, proj_weight, out_weight)))
    gathered = lax.all_to_all(packed, "ch", 0, 0, tiled=True).reshape(256, BLOCK + 128)

    sent, turned = pl.pallas_call(
        project_kernel,
        out_shape=(
            jax.ShapeDtypeStruct((PLANE * CHUNK, 128), bf16),
            jax.ShapeDtypeStruct((32, 256), bf16),
        ),
        scratch_shapes=[pltpu.VMEM((PLANE * CHUNK, 128), f32)],
        compiler_params=grant(8),
        name="project",
    )(gathered, filters)
    same_core = [[2 * c + k for c in range(PLANE)] for k in range(2)]
    mine = lax.all_to_all(
        sent.reshape(PLANE, CHUNK // 4, 4, 128),
        "seq",
        0,
        0,
        tiled=True,
        axis_index_groups=same_core,
    ).reshape(PLANE * CHUNK, 128)
    other = lax.ppermute(mine, "seq", [(i, i ^ 1) for i in range(2 * PLANE)])

    mixed = pl.pallas_call(
        convolve_kernel,
        out_shape=jax.ShapeDtypeStruct((GROUPS, 128, 128), bf16),
        scratch_shapes=[
            pltpu.VMEM((2, PLANE * CHUNK, 128), f32),
            pltpu.VMEM((128, 128), f32),
        ],
        compiler_params=grant(24),
        name="convolve",
    )(
        mine,
        other,
        short_taps,
        skip_gain,
        table["first"],
        table["last"],
        table["twiddle"],
        table["spin"],
        table["second"],
    )
    everyone = [
        [(2 * c + k) * GROUPS + z for z in range(GROUPS) for c in range(PLANE)] for k in range(2)
    ]
    arrived = lax.all_to_all(
        mixed.reshape(256, 4, 128),
        ("seq", "ch"),
        0,
        0,
        tiled=True,
        axis_index_groups=everyone,
    ).reshape(1024, 128)
    return pl.pallas_call(
        output_kernel,
        out_shape=jax.ShapeDtypeStruct((32, BLOCK), bf16),
        scratch_shapes=[pltpu.VMEM((1024, 128), f32)],
        compiler_params=grant(8),
        name="output",
    )(arrived, turned)


def solution(mesh):
    in_specs = (
        P("ch", "seq"),
        P(None, "ch", None),
        P("ch", None, None),
        P("ch", None),
        P(None, "ch", "seq"),
        P("ch", None),
    )
    return jax.shard_map(
        local, mesh=mesh, in_specs=in_specs, out_specs=P("ch", "seq"), check_vma=False
    )
```
